32 devices in a mesh: shard: 8 (over y, x, core), expert: 4 (over z).
Axes of the slice: x: 2, y: 2, z: 4, core: 2. Of those that a mesh axis runs over, the one named last changes fastest.
Arguments:
- tokens: bfloat16 [2, 4, 1024, 1024], P(None, 'expert', 'shard'), may hold values from -6 to 6
- segments: int32 [2, 4, 1024], P(None, 'expert'), may hold values from 0 to 3, never falling along the last dimension, each value on 1 to 512 neighbouring positions
- routes: int32 [2, 4, 1024, 1], P(None, 'expert', 'shard'), may hold values from 0 to 7; in each aligned block of 128 rows (0 to 127, 128 to 255, ..., all dimensions but the last counted through in order) at most 32 rows name the same one
- cotangent: bfloat16 [2, 4, 1024, 1024], P(None, 'expert', 'shard'), may hold values from -6 to 6
- norm1_gain: bfloat16 [1024], P('shard'), may hold values from 0.5 to 1.5
- qkv_weight: bfloat16 [1024, 3072], P('shard'), may hold values from -0.1875 to 0.1875
- out_weight: bfloat16 [1024, 1024], P('shard'), may hold values from -1 to 1
- norm2_gain: bfloat16 [1024], P('shard'), may hold values from 0.5 to 1.5
- mix_weight: bfloat16 [1024, 2], P('shard'), may hold values from -0.1875 to 0.1875
- dense_in: bfloat16 [1024, 4096], P('shard'), may hold values from -0.1875 to 0.1875
- dense_out: bfloat16 [4096, 1024], P('shard'), may hold values from -0.1875 to 0.1875
- expert_in: bfloat16 [8, 1024, 4096], P('expert', None, 'shard'), may hold values from -0.1875 to 0.1875
- expert_out: bfloat16 [8, 4096, 1024], P('expert', 'shard'), may hold values from -0.1875 to 0.1875
Outputs:
- output: bfloat16 [2, 4, 1024, 1024], P(None, 'expert', 'shard')
- input_grad: bfloat16 [2, 4, 1024, 1024], P(None, 'expert', 'shard')
- norm1_gain_grad: float32 [1024], P('shard')
- qkv_grad: float32 [1024, 3072], P('shard')
- out_grad: float32 [1024, 1024], P('shard')
- norm2_gain_grad: float32 [1024], P('shard')
- mix_grad: float32 [1024, 2], P('shard')
- dense_in_grad: float32 [1024, 4096], P('shard')
- dense_out_grad: float32 [4096, 1024], P('shard')
- expert_in_grad: float32 [8, 1024, 4096], P('expert', None, 'shard')
- expert_out_grad: float32 [8, 4096, 1024], P('expert', 'shard')
The draws below stay inside these ranges and needn't reach their ends.
Inputs may be any that keep to these rules, and one draw needn't show every extreme that they name: `segments`: within every sequence the numbers never fall; each document has at most 512 positions. `routes`: in each aligned block of 128 positions of a sequence and micro-batch, no expert is named more than 32 times, and in every draw some expert is named exactly 32 times in some block.
All inputs are finite; a program needn't handle non-finite values.
Results may differ from the reference program's by a relative error of at most 0.02.
Values may be sent and summed in bfloat16 or wider, within the bound.
No kernel may reach another device: no remote copies, remote signals or barrier semaphores. Data moves between devices by JAX's collectives and lax.ppermute only.
A program may use at most 176 MiB of HBM per device.

```python
import math
import jax
import jax.numpy as jnp
import numpy as np
from jax import lax

D = 1024
HEADS = 16
HEAD_DIM = 64
FF = 4096
SEQ_LEN = 1024
MB = 2
SEG_COUNT = 4
EXPERTS = 8
GROUPS = 4
TOK_MB = 128
CAP = 32


def steps_of(stream_key, extent, pieces, low, high):
    def one(dim, blocks):
        heights = jax.random.uniform(jax.random.fold_in(jax.random.fold_in(stream_key, 6), dim), (blocks,), jnp.float32, low / len(pieces), high / len(pieces))
        return jnp.repeat(jnp.exp(heights), extent[dim] // blocks).reshape((-1,) + (1,) * (len(extent) - dim - 1))

    level = one(*pieces[0])
    for cut in pieces[1:]:
        level = level * one(*cut)
    return level


def length_profile(number_of, total, limit, slope):
    loads = [(1 << 20) // math.isqrt(standing ** slope) + 1 for standing in range(2, number_of + 1)]
    surplus, holding = total - limit - (number_of - 1), [1] * (number_of - 1)
    while surplus > 0:
        movable = [i for i in range(number_of - 1) if holding[i] < limit]
        mass, remaining = sum([loads[i] for i in movable]), surplus
        for i in movable:
            addition = min(limit - holding[i], max(1, remaining * loads[i] // mass), surplus)
            holding[i] = holding[i] + addition
            surplus = surplus - addition
    return np.array([limit] + holding)


def ragged(stream_key, amount, total, reach, slope):
    if amount == 2:
        one = jax.random.randint(stream_key, (), max(1, total - reach), min(reach, total - 1) + 1)
        return jnp.stack([one, total - one])
    sizes = jnp.asarray(length_profile(amount, total, reach, slope), jnp.int32)
    couples = (amount - 1) // 2
    donor, receiver = sizes[1:1 + 2 * couples:2], sizes[2:2 + 2 * couples:2]
    slack = jnp.minimum(donor - 1, reach - receiver)
    moved = jax.random.randint(jax.random.fold_in(stream_key, 1), (couples,), 0, 1 << 20) % (slack + 1)
    sizes = sizes.at[1:1 + 2 * couples:2].set(donor - moved).at[2:2 + 2 * couples:2].set(receiver + moved)
    return sizes[jax.random.permutation(jax.random.fold_in(stream_key, 2), amount)]


def routed_block(key, own, number, rows, amount, top, limit, lean):
    ranking = jax.random.permutation(key, amount)
    packed, usual = load_shares(amount, rows * top, limit, lean, True), load_shares(amount, rows * top, limit, lean, False)
    places = jnp.arange(amount)

    def named(tallies, turn):
        used = int((tallies > 0).sum())
        fixed = max(1, used // 4)
        moved = fixed + (places - fixed + turn * (used - fixed)) % max(1, amount - fixed)
        return jnp.zeros((amount,), jnp.int32).at[ranking[jnp.where(places < fixed, places, moved)]].set(jnp.asarray(tallies, jnp.int32))

    tallies = jnp.where(number % 4 == 0, named(packed, number // 4), named(usual, number - number // 4 - 1))
    mixed = jax.random.permutation(jax.random.fold_in(own, 3), amount)
    source_of, receiver = mixed[0:amount // 2 * 2:2], mixed[1:amount // 2 * 2:2]
    margin = jnp.minimum(tallies[source_of] - 1, limit - tallies[receiver]) // 2
    margin = jnp.where((source_of == ranking[0]) | (receiver == ranking[0]) | (tallies[receiver] == 0), 0, jnp.maximum(margin, 0))
    moved = jax.random.randint(jax.random.fold_in(own, 4), (amount // 2,), 0, 1 << 20) % (margin + 1)
    tallies = tallies.at[source_of].add(-moved).at[receiver].add(moved)
    items = jnp.searchsorted(jnp.cumsum(tallies), jnp.arange(rows * top), side="right").astype(jnp.int32)
    grid = items.reshape(top, rows).T
    grid = grid[jax.random.permutation(jax.random.fold_in(own, 1), rows)]
    turn = jax.random.randint(jax.random.fold_in(own, 2), (rows, 1), 0, top)
    return jnp.take_along_axis(grid, (jnp.arange(top)[None, :] + turn) % top, axis=1)


def load_shares(count, total, limit, slope, full):
    weights = [(1 << 20) // math.isqrt(rank ** slope) + 1 for rank in range(1, count + 1)]
    largest = limit if full else min(limit, max(-(-total // count), total * weights[0] // sum(weights)))
    least = 1 if total - largest >= count - 1 else 0
    counts, spare = [largest] + [least] * (count - 1), total - largest - least * (count - 1)
    while spare > 0:
        candidates = [i for i in range(1, count) if counts[i] < largest] or [i for i in range(1, count) if counts[i] < limit]
        whole, budget = sum([weights[i] for i in candidates]), spare
        for i in candidates:
            more = min(limit - counts[i], max(1, budget * weights[i] // whole), spare)
            counts[i] = counts[i] + more
            spare = spare - more
    return np.array(counts)


def noise(rng, shape, scale, limit, pieces=(), held_as=jnp.bfloat16):
    drawn = jax.random.normal(rng, shape, jnp.float32) * scale
    if len(pieces) > 0:
        drawn = steps_of(rng, shape, pieces, -0.22, 0.18) * drawn
    return jnp.clip(drawn, min=-limit, max=limit).astype(held_as)


def setup_inputs(seed: int = 0) -> dict:
    key_list = jax.random.split(jax.random.key(seed), 14)
    tokens = noise(key_list[0], (MB, GROUPS, SEQ_LEN, D), 1.0, 6.0, ((1, 4), (2, 8)))
    segments = jax.vmap(lambda own: jnp.searchsorted(jnp.cumsum(ragged(own, SEG_COUNT, SEQ_LEN, SEQ_LEN // 2, 2)), jnp.arange(SEQ_LEN), side="right"))(jax.random.split(key_list[1], MB * GROUPS)).reshape((MB, GROUPS, SEQ_LEN)).astype(jnp.int32)
    routes_keys = jax.random.split(jax.random.fold_in(key_list[2], 1), MB * GROUPS * SEQ_LEN // TOK_MB)
    routes_turns = jax.random.permutation(jax.random.fold_in(key_list[2], 3), MB * GROUPS * SEQ_LEN // TOK_MB)
    routes = jax.vmap(lambda own, number: routed_block(jax.random.fold_in(key_list[2], 2), own, number, TOK_MB, EXPERTS, 1, CAP, 2))(routes_keys, routes_turns).reshape((MB, GROUPS, SEQ_LEN, 1))
    cotangent = noise(key_list[3], (MB, GROUPS, SEQ_LEN, D), 1.0, 6.0, ((1, 4), (2, 8)))
    norm1_gain = jnp.clip(1.0 + 0.1 * jax.random.normal(key_list[4], (D,), jnp.float32), 0.5, 1.5).astype(jnp.bfloat16)
    qkv_weight = noise(key_list[5], (D, 3 * D), D ** -0.5, 0.1875, ((0, 8),))
    out_weight = noise(key_list[6], (D, D), (D // 32) ** -0.5, 1.0, ((0, 8),))
    norm2_gain = jnp.clip(1.0 + 0.1 * jax.random.normal(key_list[7], (D,), jnp.float32), 0.5, 1.5).astype(jnp.bfloat16)
    mix_weight = noise(key_list[8], (D, 2), D ** -0.5, 0.1875, ((0, 8),))
    dense_in = noise(key_list[9], (D, FF), D ** -0.5, 0.1875, ((0, 8),))
    dense_out = noise(key_list[10], (FF, D), (FF // 4) ** -0.5, 0.1875, ((0, 8),))
    expert_in = noise(key_list[11], (EXPERTS, D, FF), D ** -0.5, 0.1875, ((0, 4), (2, 8)))
    expert_out = noise(key_list[12], (EXPERTS, FF, D), (FF // 4) ** -0.5, 0.1875, ((0, 4), (1, 8)))
    return {"tokens": tokens, "segments": segments, "routes": routes, "cotangent": cotangent, "norm1_gain": norm1_gain, "qkv_weight": qkv_weight, "out_weight": out_weight, "norm2_gain": norm2_gain, "mix_weight": mix_weight, "dense_in": dense_in, "dense_out": dense_out, "expert_in": expert_in, "expert_out": expert_out}


@jax.custom_vjp
def low(v):
    return lax.optimization_barrier(v.astype(jnp.bfloat16)).astype(jnp.float32)

@jax.custom_vjp
def low_back(v):
    return v

def low_keep(v):
    return (low(v), None)

def low_pass(kept, grad):
    return (grad,)

def back_keep(v):
    return (v, None)

def back_low(kept, grad):
    return (low(grad),)
low.defvjp(low_keep, low_pass)
low_back.defvjp(back_keep, back_low)

def layer_norm(values, gain):
    center = lax.optimization_barrier(jnp.mean(values, axis=-1, keepdims=True))
    shifted = values - center
    spread = lax.optimization_barrier(jnp.mean(shifted * shifted, axis=-1, keepdims=True))
    return shifted * lax.rsqrt(spread + 1e-05) * gain

def activate(values):
    return jax.nn.gelu(values, approximate=True)

def reference(tokens, segments, routes, cotangent, norm1_gain, qkv_weight, out_weight, norm2_gain, mix_weight, dense_in, dense_out, expert_in, expert_out):
    highest = lax.Precision.HIGHEST
    n_seq = MB * GROUPS
    group = math.gcd(n_seq, max(1, 4096 // SEQ_LEN))
    n_blocks = n_seq // group
    n_rows = n_seq * SEQ_LEN
    seg_blocks = segments.reshape(n_blocks, group, SEQ_LEN)
    flat_routes = routes.reshape(-1).astype(jnp.int32)
    dev_blocks = n_rows // TOK_MB
    onehot = (flat_routes.reshape(dev_blocks, TOK_MB)[:, :, None] == jnp.arange(EXPERTS, dtype=jnp.int32)[None, None, :]).astype(jnp.int32)
    rank = lax.optimization_barrier(jnp.sum((jnp.cumsum(onehot, axis=1) - onehot) * onehot, axis=2)).reshape(-1)
    block_id = jnp.arange(n_rows, dtype=jnp.int32) // TOK_MB
    slot = (block_id * CAP + rank).astype(jnp.int32)
    span = dev_blocks * CAP
    scale = HEAD_DIM ** (-0.5)
    positions = jnp.arange(SEQ_LEN, dtype=jnp.int32)
    causal = positions[None, :] <= positions[:, None]

    def forward(inputs, gain_one, w_qkv, w_attn, gain_two, w_mix, w_in, w_down, e_in, e_down):

        def attend(pair):
            block_x, block_seg = pair
            normed = low(layer_norm(block_x, gain_one))
            qkv = low(low_back(jnp.einsum('gsd,de->gse', normed, w_qkv, precision=highest)))
            queries = qkv[..., :D].reshape(group, SEQ_LEN, HEADS, HEAD_DIM)
            keys = qkv[..., D:2 * D].reshape(group, SEQ_LEN, HEADS, HEAD_DIM)
            values = qkv[..., 2 * D:].reshape(group, SEQ_LEN, HEADS, HEAD_DIM)
            scores = low_back(jnp.einsum('gqhd,gkhd->ghqk', queries, keys, precision=highest) * scale)
            allowed = (causal[None] & (block_seg[:, :, None] == block_seg[:, None, :]))[:, None]
            masked = jnp.where(allowed, scores, -1e+30)
            row_max = lax.optimization_barrier(jnp.max(masked, axis=-1, keepdims=True))
            weights_exp = jnp.where(allowed, jnp.exp(scores - row_max), 0.0)
            probs = weights_exp / lax.optimization_barrier(jnp.sum(weights_exp, axis=-1, keepdims=True))
            heads = low(low_back(jnp.einsum('ghqk,gkhd->gqhd', low(probs), values, precision=highest)))
            heads = heads.reshape(group, SEQ_LEN, D)
            return block_x + low_back(jnp.einsum('gsd,de->gse', heads, w_attn, precision=highest))
        blocks_x = inputs.reshape(n_blocks, group, SEQ_LEN, D)
        mid = lax.map(jax.checkpoint(attend), (blocks_x, seg_blocks)).reshape(n_rows, D)
        normed_two = low(layer_norm(mid, gain_two))

        def dense(block_rows):
            dense_up = low_back(jnp.dot(block_rows, w_in, precision=highest))
            return low_back(jnp.dot(low(activate(dense_up)), w_down, precision=highest))
        dense_branch = lax.map(jax.checkpoint(dense), normed_two.reshape(n_blocks, group * SEQ_LEN, D)).reshape(n_rows, D)
        mixing = jax.nn.softmax(jnp.dot(normed_two, w_mix, precision=highest), axis=-1)
        buffer = jnp.zeros((EXPERTS, span, D), jnp.float32).at[flat_routes, slot].set(normed_two)
        buffer = low_back(buffer)

        def run_expert(triple):
            rows_e, first, second = triple
            expert_up = low_back(jnp.dot(rows_e, first, precision=highest))
            return low(low_back(jnp.dot(low(activate(expert_up)), second, precision=highest)))
        results = lax.map(jax.checkpoint(run_expert), (buffer, e_in, e_down))
        expert_branch = results[flat_routes, slot]
        mixed = mid + mixing[:, 0:1] * dense_branch + mixing[:, 1:2] * expert_branch
        return mixed.reshape(inputs.shape)
    primals = (tokens.astype(jnp.float32), norm1_gain.astype(jnp.float32), qkv_weight.astype(jnp.float32), out_weight.astype(jnp.float32), norm2_gain.astype(jnp.float32), mix_weight.astype(jnp.float32), dense_in.astype(jnp.float32), dense_out.astype(jnp.float32), expert_in.astype(jnp.float32), expert_out.astype(jnp.float32))
    result, pullback = jax.vjp(forward, *primals)
    grads = pullback(cotangent.astype(jnp.float32))
    return (result.astype(jnp.bfloat16), grads[0].astype(jnp.bfloat16), grads[1], grads[2], grads[3], grads[4], grads[5], grads[6], grads[7], grads[8], grads[9])
```

```python
import functools

import jax
import jax.numpy as jnp
import numpy as np
from jax import lax
from jax.experimental import pallas as pl
from jax.experimental.pallas import tpu as pltpu
from jax.sharding import PartitionSpec as P

HEADS = 16
HEAD_DIM = 64
F32 = jnp.float32
BF16 = jnp.bfloat16
GELU_A = 0.7978845608028654
GELU_B = 0.044715


def layer_norm(values, gain):
    center = jnp.mean(values, axis=-1, keepdims=True)
    shifted = values - center
    spread = jnp.mean(shifted * shifted, axis=-1, keepdims=True)
    return shifted * lax.rsqrt(spread + 1e-05) * gain


def bit_order(half, n):
    bits = [1 << i for i in range(n.bit_length() - 1)]
    rest = bits[1:]
    return (rest if half % 2 == 0 else rest[::-1]) + bits[:1]


def offsets(half, n):
    order = bit_order(half, n)
    return [sum(b for s, b in enumerate(order) if j >> s & 1) for j in range(n)]


def swap(x, bit, n):
    return lax.ppermute(x, "shard", [(i, i ^ bit) for i in range(n)])


def gather_rows(halves, n):
    held = list(halves)
    steps = n.bit_length() - 1
    for step in range(steps):
        got = [swap(x, bit_order(h, n)[step], n) for h, x in enumerate(held)]
        if step == steps - 1:
            return jnp.concatenate([y for pair in zip(held, got) for y in pair], axis=0)
        held = [jnp.concatenate(pair, axis=0) for pair in zip(held, got)]
    return jnp.concatenate(held, axis=0)


def scatter_sum(halves, n):
    held = list(halves)
    steps = n.bit_length() - 1
    for step in reversed(range(steps)):
        nxt = []
        for h, x in enumerate(held):
            size = x.shape[0] // 2
            got = swap(x[size:], bit_order(h, n)[step], n)
            nxt.append((x[:size].astype(F32) + got.astype(F32)).astype(BF16))
        held = nxt
    return held


def natural(order_ref, src_ref, dst_ref, n, rows):
    m = pl.program_id(0)
    for i in range(n):
        at = pl.multiple_of(order_ref[m, i] * rows, rows)
        dst_ref[i * rows : (i + 1) * rows, :] = src_ref[0, pl.ds(at, rows), :]


def of_head(x, h):
    lane = lax.broadcasted_iota(jnp.int32, x.shape, 1)
    return jnp.where(lane // HEAD_DIM == h, x, jnp.zeros_like(x))


def dot(a, b, ca, cb):
    return lax.dot_general(a, b, (((ca,), (cb,)), ((), ())), preferred_element_type=F32)


def attend_body(n, rows, hd, bq, order_ref, qkv_ref, segr_ref, segc_ref, out_ref, qkv_s):
    natural(order_ref, qkv_ref, qkv_s, n, rows)
    scale = HEAD_DIM ** (-0.5)
    for b in range(n * rows // bq):
        lo, hi = b * bq, (b + 1) * bq
        q, k, v = qkv_s[lo:hi, :hd], qkv_s[:hi, hd : 2 * hd], qkv_s[:hi, 2 * hd :]
        qpos = lo + lax.broadcasted_iota(jnp.int32, (bq, hi), 0)
        kpos = lax.broadcasted_iota(jnp.int32, (bq, hi), 1)
        allowed = (kpos <= qpos) & (segc_ref[0, lo:hi, :] == segr_ref[0, :, :hi])
        out = jnp.zeros((bq, hd), F32)
        for h in range(hd // HEAD_DIM):
            scores = dot(of_head(q, h), k, 1, 1) * scale
            top = jnp.max(jnp.where(allowed, scores, -1e30), axis=1, keepdims=True)
            e = jnp.where(allowed, jnp.exp(scores - top), 0.0)
            p = e / jnp.sum(e, axis=1, keepdims=True)
            out = out + of_head(dot(p.astype(BF16), v, 1, 0), h)
        out = out.astype(BF16)
        for i in range(bq // rows):
            out_ref[lo // rows + i, 0] = out[i * rows : (i + 1) * rows, :]


def attend_back_body(
    n, rows, hd, bq, order_ref, qkv_ref, go_ref, segr_ref, segc_ref, out_ref, qkv_s, acc_s
):
    natural(order_ref, qkv_ref, qkv_s, n, rows)
    m = pl.program_id(0)
    scale = HEAD_DIM ** (-0.5)
    acc_s[...] = jnp.zeros_like(acc_s)
    for b in range(n * rows // bq):
        lo, hi = b * bq, (b + 1) * bq
        q, k, v = qkv_s[lo:hi, :hd], qkv_s[:hi, hd : 2 * hd], qkv_s[:hi, 2 * hd :]
        go = jnp.concatenate([go_ref[lo // rows + i, 0] for i in range(bq // rows)], axis=0)
        kpos = lax.broadcasted_iota(jnp.int32, (hi, bq), 0)
        qpos = lo + lax.broadcasted_iota(jnp.int32, (hi, bq), 1)
        allowed = (kpos <= qpos) & (segc_ref[0, :hi, :] == segr_ref[0, :, lo:hi])
        dq = jnp.zeros((bq, hd), F32)
        dk = jnp.zeros((hi, hd), F32)
        dv = jnp.zeros((hi, hd), F32)
        for h in range(hd // HEAD_DIM):
            scores = dot(k, of_head(q, h), 1, 1) * scale
            top = jnp.max(jnp.where(allowed, scores, -1e30), axis=0, keepdims=True)
            e = jnp.where(allowed, jnp.exp(scores - top), 0.0)
            p = e / jnp.sum(e, axis=0, keepdims=True)
            dp = dot(v, of_head(go, h), 1, 1)
            delta = jnp.sum(p * dp, axis=0, keepdims=True)
            ds = (p * (dp - delta)).astype(BF16)
            dq = dq + of_head(dot(ds, k, 0, 0), h)
            dk = dk + of_head(dot(ds, q, 1, 0), h)
            dv = dv + of_head(dot(p.astype(BF16), go, 1, 0), h)
        acc_s[lo:hi, :hd] = dq * scale
        acc_s[:hi, hd : 2 * hd] += dk * scale
        acc_s[:hi, 2 * hd :] += dv
    for i in range(n):
        at = pl.multiple_of(order_ref[m, i] * rows, rows)
        out_ref[0, pl.ds(at, rows), :] = acc_s[i * rows : (i + 1) * rows, :].astype(BF16)


def attend(order, qkv, segments, n, rows, hd, grad_heads=None):
    micro, seq, cols = qkv.shape
    segr, segc = segments[:, None, :], segments[:, :, None]
    bq = min(seq, 256)
    flat = pl.BlockSpec((1, seq, cols), lambda m, o: (m, 0, 0))
    heads = pl.BlockSpec((n, 1, rows, hd), lambda m, o: (0, m, 0, 0))
    segs = [
        pl.BlockSpec((1, 1, seq), lambda m, o: (m, 0, 0)),
        pl.BlockSpec((1, seq, 1), lambda m, o: (m, 0, 0)),
    ]
    scratch = [pltpu.VMEM((seq, cols), BF16)]
    area = micro * seq * seq * (hd // HEAD_DIM)
    if grad_heads is None:
        return pl.pallas_call(
            functools.partial(attend_body, n, rows, hd, bq),
            out_shape=jax.ShapeDtypeStruct((n, micro, rows, hd), BF16),
            grid_spec=pltpu.PrefetchScalarGridSpec(
                num_scalar_prefetch=1,
                grid=(micro,),
                in_specs=[flat] + segs,
                out_specs=heads,
                scratch_shapes=scratch,
            ),
            name="attend",
            cost_estimate=pl.CostEstimate(
                flops=area * 512, transcendentals=area, bytes_accessed=qkv.size * 3
            ),
        )(order, qkv, segr, segc)
    return pl.pallas_call(
        functools.partial(attend_back_body, n, rows, hd, bq),
        out_shape=jax.ShapeDtypeStruct((micro, seq, cols), BF16),
        grid_spec=pltpu.PrefetchScalarGridSpec(
            num_scalar_prefetch=1,
            grid=(micro,),
            in_specs=[flat, heads] + segs,
            out_specs=flat,
            scratch_shapes=scratch + [pltpu.VMEM((seq, cols), F32)],
        ),
        name="attend_back",
        cost_estimate=pl.CostEstimate(
            flops=area * 1280, transcendentals=area, bytes_accessed=qkv.size * 6
        ),
    )(order, qkv, grad_heads, segr, segc)


def ffn_body(branch, x_ref, c_ref, wi_ref, wo_ref, wm_ref, yd_ref, gi_ref, go_ref):
    width = x_ref.shape[1]
    x = x_ref[...]
    wi, wo = wi_ref[...], wo_ref[...]
    logits = dot(x, wm_ref[...], 1, 0)
    first, second = logits[:, 0:1], logits[:, 1:2]
    top = jnp.maximum(first, second)
    first, second = jnp.exp(first - top), jnp.exp(second - top)
    mix = (second if branch else first) / (first + second)
    g = (mix * c_ref[...].astype(F32)).astype(BF16)
    up = dot(x, wi, 1, 0)
    t = jnp.tanh(GELU_A * (up + GELU_B * (up * up * up)))
    act = (0.5 * up * (1.0 + t)).astype(BF16)
    slope = 0.5 * (1.0 + t) + 0.5 * up * (1.0 - t * t) * (GELU_A * (1.0 + 3.0 * GELU_B * up * up))
    yd_ref[:, :width] = dot(act, wo, 1, 0).astype(BF16)
    dup = (dot(g, wo, 1, 1) * slope).astype(BF16)
    yd_ref[:, width:] = dot(dup, wi, 1, 1).astype(BF16)
    gi = dot(x, dup, 0, 0)
    go = dot(act, g, 0, 0)

    @pl.when(pl.program_id(0) == 0)
    def _():
        gi_ref[...] = gi
        go_ref[...] = go

    @pl.when(pl.program_id(0) > 0)
    def _():
        gi_ref[...] += gi
        go_ref[...] += go


def ffn(branch, x, c, w_in, w_out, mix_pad):
    count, width = x.shape
    units = w_in.shape[1]
    block = min(count, 512)
    row = lambda cols: pl.BlockSpec((block, cols), lambda b: (b, 0))
    whole = lambda a: pl.BlockSpec(a, lambda b: (0, 0))
    return pl.pallas_call(
        functools.partial(ffn_body, branch),
        out_shape=(
            jax.ShapeDtypeStruct((count, 2 * width), BF16),
            jax.ShapeDtypeStruct((width, units), F32),
            jax.ShapeDtypeStruct((units, width), F32),
        ),
        grid=(count // block,),
        in_specs=[
            row(width),
            row(width),
            whole(w_in.shape),
            whole(w_out.shape),
            whole(mix_pad.shape),
        ],
        out_specs=(row(2 * width), whole(w_in.shape), whole(w_out.shape)),
        name="ffn",
        compiler_params=pltpu.CompilerParams(vmem_limit_bytes=56 * 1024 * 1024),
        cost_estimate=pl.CostEstimate(
            flops=12 * count * width * units,
            transcendentals=count * units,
            bytes_accessed=8 * count * width + 12 * width * units,
        ),
    )(x, c, w_in, w_out, mix_pad)


def per_device(
    tokens,
    segments,
    routes,
    cotangent,
    norm1_gain,
    qkv_weight,
    out_weight,
    norm2_gain,
    mix_weight,
    dense_in,
    dense_out,
    expert_in,
    expert_out,
):
    highest = lax.Precision.HIGHEST
    micro, _, rows, width = tokens.shape
    n = lax.axis_size("shard")
    n_expert = lax.axis_size("expert")
    me = lax.axis_index("shard")
    seq = segments.shape[2]
    hd = width // n
    local = expert_in.shape[0]
    experts = local * n_expert
    capacity = max(2, 2 * rows // experts)
    wrow = qkv_weight.shape[0]
    segs = segments[:, 0]
    x_in = tokens[:, 0]
    cot = cotangent[:, 0]
    table = np.array(
        [[[offsets(m, n).index(i ^ d) for i in range(n)] for m in range(micro)] for d in range(n)],
        np.int32,
    )
    order = jnp.asarray(table)[me]

    tokens_all = gather_rows([x_in[m] for m in range(micro)], n)
    small = jnp.concatenate([norm1_gain[None], norm2_gain[None], mix_weight.T], axis=0)
    small_all = lax.all_gather(small, "shard", axis=0).transpose(1, 0, 2).reshape(4, width)
    gain_one, gain_two = small_all[0].astype(F32), small_all[1].astype(F32)
    mix_full = small_all[2:].T
    mix_pad = jnp.pad(mix_full, ((0, 0), (0, 126)))
    wq = qkv_weight.reshape(wrow, 3, n, hd).transpose(2, 0, 1, 3).reshape(n, wrow, 3 * hd)
    wq = lax.all_to_all(wq, "shard", split_axis=0, concat_axis=0, tiled=True)
    wq = wq.reshape(width, 3 * hd)
    wo_full = lax.all_gather(out_weight, "shard", axis=0, tiled=True)
    units = dense_in.shape[1] // n
    w_in = dense_in.reshape(wrow, n, units).transpose(1, 0, 2)
    w_in = lax.all_to_all(w_in, "shard", split_axis=0, concat_axis=0, tiled=True)
    w_in = w_in.reshape(width, units)

    route = routes[:, 0, :, 0]
    onehot = (route[:, :, None] == jnp.arange(experts, dtype=jnp.int32)).astype(jnp.int32)
    rank = jnp.sum((jnp.cumsum(onehot, axis=1) - onehot) * onehot, axis=2)
    slot = route * capacity + rank
    slot_ids = jnp.arange(experts * capacity, dtype=jnp.int32)
    placing = (slot[:, None, :] == slot_ids[None, :, None]).astype(BF16)

    def dispatch(values):
        sent = jnp.einsum("mst,mtd->msd", placing, values, preferred_element_type=F32).astype(BF16)
        sent = sent.reshape(micro, n_expert, local, capacity, width).transpose(1, 2, 0, 3, 4)
        got = lax.all_to_all(sent, "expert", split_axis=0, concat_axis=0, tiled=True)
        got = got.transpose(1, 2, 0, 3, 4).reshape(local, micro, n_expert * capacity, width)
        return [gather_rows([got[j, m] for m in range(micro)], n) for j in range(local)]

    cot_all = gather_rows([cot[m] for m in range(micro)], n)
    cot_rows = dispatch(cot)

    wide = tokens_all.astype(F32)
    center = jnp.mean(wide, axis=-1, keepdims=True)
    shifted = wide - center
    spread = jnp.mean(shifted * shifted, axis=-1, keepdims=True)
    unit_all = shifted * lax.rsqrt(spread + 1e-05)
    normed_all = (unit_all * gain_one).astype(BF16)
    qkv = jnp.dot(normed_all, wq, preferred_element_type=F32).astype(BF16)
    qkv = qkv.reshape(micro, seq, 3 * hd)
    heads = attend(order, qkv, segs, n, rows, hd)
    heads = lax.all_to_all(heads, "shard", split_axis=0, concat_axis=0, tiled=True)
    heads_out = heads.transpose(1, 2, 0, 3).reshape(micro * rows, width)
    inputs = x_in.reshape(micro * rows, width).astype(F32)
    mid = inputs + jnp.dot(heads_out, wo_full, preferred_element_type=F32)

    normed_t, norm_two_back = jax.vjp(layer_norm, mid, gain_two)
    normed_two = normed_t.astype(BF16)
    by_half = normed_two.reshape(micro, rows, width)
    x_all = gather_rows([by_half[m] for m in range(micro)], n)
    x_rows = dispatch(by_half)

    def split(values):
        return [values[m * (values.shape[0] // micro) :][: values.shape[0] // micro] for m in range(micro)]

    part, in_grad, down_grad = ffn(0, x_all, cot_all, w_in, dense_out, mix_pad)
    dense_sum = jnp.concatenate(scatter_sum(split(part), n), axis=0).astype(F32)
    in_grad = in_grad.reshape(n, wrow, units).astype(BF16)
    in_grad = lax.all_to_all(in_grad, "shard", split_axis=0, concat_axis=0, tiled=True)
    in_grad = in_grad.transpose(1, 0, 2).reshape(wrow, n * units)
    in_total = lax.psum(in_grad, "expert").astype(F32)
    down_total = lax.psum(down_grad.astype(BF16), "expert").astype(F32)

    sums, e_in_grads, e_out_grads = [], [], []
    for j in range(local):
        part, gi, go = ffn(1, x_rows[j], cot_rows[j], expert_in[j], expert_out[j], mix_pad)
        sums.append(jnp.stack(scatter_sum(split(part), n)))
        e_in_grads.append(gi)
        e_out_grads.append(go)
    back = jnp.stack(sums).reshape(local, micro, n_expert, capacity, 2 * width)
    back = lax.all_to_all(
        back.transpose(2, 0, 1, 3, 4), "expert", split_axis=0, concat_axis=0, tiled=True
    )
    back = back.transpose(2, 0, 1, 3, 4).reshape(micro, experts * capacity, 2 * width)
    expert_sum = jnp.einsum("mst,msd->mtd", placing, back, preferred_element_type=F32)
    expert_sum = expert_sum.reshape(micro * rows, 2 * width)

    logits = jnp.dot(normed_two, mix_full, preferred_element_type=F32)
    mixing, mixing_back = jax.vjp(lambda values: jax.nn.softmax(values, axis=-1), logits)
    dense_branch, expert_branch = dense_sum[:, :width], expert_sum[:, :width]
    output = (mid + mixing[:, 0:1] * dense_branch + mixing[:, 1:2] * expert_branch).astype(BF16)
    grad_y = cot.reshape(micro * rows, width).astype(F32)
    grad_mix_c = jnp.stack(
        [jnp.sum(grad_y * dense_branch, axis=-1), jnp.sum(grad_y * expert_branch, axis=-1)],
        axis=-1,
    )
    grad_logits = mixing_back(grad_mix_c)[0]
    grad_mix = jnp.einsum("td,tc->dc", normed_two.astype(F32), grad_logits, precision=highest)
    grad_normed_two = (
        dense_sum[:, width:]
        + expert_sum[:, width:]
        + jnp.einsum("tc,dc->td", grad_logits, mix_full.astype(F32), precision=highest)
    )
    grad_mid_norm, grad_two = norm_two_back(grad_normed_two)
    grad_mid = grad_y + grad_mid_norm

    grad_attn = grad_mid.astype(BF16)
    grad_heads = jnp.einsum("te,de->td", grad_attn, wo_full, preferred_element_type=F32)
    grad_heads = grad_heads.astype(BF16).reshape(micro, rows, n, hd).transpose(2, 0, 1, 3)
    grad_heads = lax.all_to_all(grad_heads, "shard", split_axis=0, concat_axis=0, tiled=True)
    grad_wo = jnp.einsum("td,te->de", heads_out, grad_attn, preferred_element_type=F32)
    tail = jnp.concatenate([grad_two[None], grad_mix.T], axis=0).reshape(3, n, wrow)
    tail = tail.transpose(1, 0, 2).reshape(n, 1, 3 * wrow)
    tail = jnp.pad(tail, ((0, 0), (0, 15), (0, width - 3 * wrow)))
    grad_wo = jnp.concatenate([grad_wo.reshape(n, wrow, width), tail], axis=1).astype(BF16)
    grad_wo = lax.psum_scatter(grad_wo, "shard", scatter_dimension=0, tiled=True)[0]

    grad_qkv = attend(order, qkv, segs, n, rows, hd, grad_heads).reshape(micro * seq, 3 * hd)
    grad_normed_one = jnp.einsum("te,de->td", grad_qkv, wq, preferred_element_type=F32)
    gain_one_part = jnp.sum(grad_normed_one * unit_all, axis=0)
    first = scatter_sum(split(grad_normed_one.astype(BF16)), n)
    first = jnp.concatenate(first, axis=0).astype(F32)
    _, norm_one_back = jax.vjp(lambda v: layer_norm(v, gain_one), inputs)
    input_grad = (grad_mid + norm_one_back(first)[0]).astype(BF16)
    grad_wq = jnp.einsum("td,te->de", normed_all, grad_qkv, preferred_element_type=F32)
    grad_wq = grad_wq.reshape(n, wrow, 3 * hd)
    ones = jnp.pad(gain_one_part.reshape(n, 1, wrow), ((0, 0), (0, 15), (0, 3 * hd - wrow)))
    grad_wq = jnp.concatenate([grad_wq, ones], axis=1).astype(BF16)
    grad_wq = lax.all_to_all(grad_wq, "shard", split_axis=0, concat_axis=0, tiled=True)
    gain_one_grad = jnp.sum(grad_wq[:, wrow, :wrow].astype(F32), axis=0)
    grad_wq = grad_wq[:, :wrow].reshape(n, wrow, 3, hd).transpose(1, 2, 0, 3)
    grad_wq = grad_wq.reshape(wrow, 3 * width)

    wq_total = lax.psum(grad_wq, "expert").astype(F32)
    wo_total = lax.psum(grad_wo[:wrow], "expert").astype(F32)
    vectors = jnp.concatenate([grad_wo[wrow, : 3 * wrow].astype(F32), gain_one_grad])
    vectors = lax.psum(vectors, "expert").reshape(4, wrow)

    return (
        output.reshape(micro, 1, rows, width),
        input_grad.reshape(micro, 1, rows, width),
        vectors[3],
        wq_total,
        wo_total,
        vectors[0],
        vectors[1:3].T,
        in_total,
        down_total,
        jnp.stack(e_in_grads),
        jnp.stack(e_out_grads),
    )


def solution(mesh):
    return jax.shard_map(
        per_device,
        mesh=mesh,
        in_specs=(
            P(None, "expert", "shard", None),
            P(None, "expert", None),
            P(None, "expert", "shard", None),
            P(None, "expert", "shard", None),
            P("shard"),
            P("shard", None),
            P("shard", None),
            P("shard"),
            P("shard", None),
            P("shard", None),
            P("shard", None),
            P("expert", None, "shard"),
            P("expert", "shard", None),
        ),
        out_specs=(
            P(None, "expert", "shard", None),
            P(None, "expert", "shard", None),
            P("shard"),
            P("shard", None),
            P("shard", None),
            P("shard"),
            P("shard", None),
            P("shard", None),
            P("shard", None),
            P("expert", None, "shard"),
            P("expert", "shard", None),
        ),
        check_vma=False,
    )
```
